32 devices in a mesh: lat: 4 (over y, x), lon: 8 (over z, core).
Axes of the slice: x: 2, y: 2, z: 4, core: 2. Of those that a mesh axis runs over, the one named last changes fastest.
Arguments:
- wind_u: float32 [32, 32, 1024], P(None, 'lat', 'lon'), may hold values from -6 to 6
- wind_v: float32 [32, 32, 1024], P(None, 'lat', 'lon'), may hold values from -6 to 6
Outputs:
- modes: float32 [32, 2, 32, 1024], P(None, None, 'lat', 'lon')
- factor: float32 [32, 32], replicated
The draws below stay inside these ranges and needn't reach their ends.
All inputs are finite; a program needn't handle non-finite values.
Results may differ from the reference program's by a relative error of at most 0.0003.
Values sent between devices are 32-bit elements; how exact they have to be, the bound alone decides.
A program may use at most 64 MiB of HBM per device.

```python
import math
import jax
import jax.numpy as jnp
from jax import lax

SNAPS = 32
NLAT = 32
NLON = 1024
ROWS = 65536


def wind_field(key, offset):
    keys = [jax.random.fold_in(key, offset + number) for number in range(4)]
    lat_frac = jnp.arange(NLAT).astype(jnp.float32) / NLAT
    lon_frac = jnp.arange(NLON).astype(jnp.float32) / NLON
    noise = jax.random.normal(keys[0], (SNAPS, NLAT, NLON), jnp.float32)
    ramp = 3.0 ** (0.5 * lat_frac[:, None] + 0.5 * lon_frac[None, :])
    base = jax.random.uniform(keys[1], (NLAT, NLON), jnp.float32, -1.2, 1.2)
    cells = jnp.exp(jax.random.uniform(keys[2], (NLAT, NLON), jnp.float32, 0.0, math.log(3.4)))
    raw_snaps = jnp.exp(jax.random.uniform(keys[3], (SNAPS, 1, 1), jnp.float32, 0.0, math.log(10.0)))
    snaps = raw_snaps / jnp.min(raw_snaps)
    field = 0.025 * snaps * (ramp * cells)[None, :, :] * (base[None, :, :] + noise / 30.0)
    return jnp.clip(field, -6.0, 6.0)


def draw_wind_u(key, part):
    return wind_field(key, 100)


def draw_wind_v(key, part):
    return wind_field(key, 200)


def setup_inputs(seed: int = 0) -> dict:
    seeds = jax.random.split(jax.random.key(seed), 3)
    wind_u = draw_wind_u(jax.random.fold_in(seeds[2], 71), 0)
    wind_v = draw_wind_v(jax.random.fold_in(seeds[2], 71), 0)
    return {"wind_u": wind_u, "wind_v": wind_v}


def upper_factor(gram):
    count = gram.shape[0]
    positions = jnp.arange(count)

    def column_step(k, state):
        rest, lower = state
        onehot = (positions == k).astype(jnp.float32)
        below = (positions >= k).astype(jnp.float32)
        pivot = jnp.sum(rest * onehot[:, None] * onehot[None, :])
        column = lax.optimization_barrier(jnp.sum(rest * onehot[None, :], axis=1)) * below / jnp.sqrt(pivot)
        lower = lower + column[:, None] * onehot[None, :]
        rest = rest - column[:, None] * column[None, :]
        return (rest, lower)
    start = (gram.astype(jnp.float32), jnp.zeros(gram.shape, jnp.float32))
    rest, lower = lax.fori_loop(0, count, column_step, start)
    return lower.T

def inverse_upper(upper):
    count = upper.shape[0]
    positions = jnp.arange(count)

    def row_step(i, result):
        k = count - 1 - i
        onehot = (positions == k).astype(jnp.float32)
        row_of = lax.optimization_barrier(jnp.sum(upper * onehot[:, None], axis=0))
        diag = jnp.sum(row_of * onehot)
        off_diag = row_of * (1.0 - onehot)
        new_row = (onehot - lax.optimization_barrier(jnp.sum(off_diag[:, None] * result, axis=0))) / diag
        return result + onehot[:, None] * new_row[None, :]
    return lax.fori_loop(0, count, row_step, jnp.zeros(upper.shape, jnp.float32))

def build_columns(wind_u, wind_v):
    step = 2.0 * math.pi / NLON
    index = jnp.arange(NLAT).astype(jnp.float32)
    cosines = jnp.cos((index + 0.5 - NLAT / 2) * step)
    weight_c = cosines[None, :, None]

    def lat_diff(field):
        padded = jnp.pad(field * weight_c, ((0, 0), (1, 1), (0, 0)))
        return padded[:, 2:, :] - padded[:, :-2, :]

    def lon_diff(field):
        return jnp.roll(field, -1, axis=2) - jnp.roll(field, 1, axis=2)
    scale = (0.5 / jnp.sqrt(cosines))[None, :, None]
    vorticity = (lon_diff(wind_v) - lat_diff(wind_u)) * scale
    divergence = (lon_diff(wind_u) + lat_diff(wind_v)) * scale
    return jnp.stack([vorticity, divergence], axis=1)

def reference(wind_u, wind_v):
    highest = lax.Precision.HIGHEST
    block = build_columns(wind_u, wind_v).reshape(SNAPS, -1)
    gram_one = jnp.dot(block, block.T, precision=highest, preferred_element_type=jnp.float32)
    first = upper_factor(gram_one)
    solved = jnp.dot(inverse_upper(first).T, block, precision=highest, preferred_element_type=jnp.float32)
    gram_two = jnp.dot(solved, solved.T, precision=highest, preferred_element_type=jnp.float32)
    second = upper_factor(gram_two)
    root = math.sqrt(ROWS)
    modes = jnp.dot(inverse_upper(second).T, solved, precision=highest, preferred_element_type=jnp.float32) * root
    factor = jnp.dot(second, first, precision=highest, preferred_element_type=jnp.float32) / root
    return (modes.reshape(SNAPS, 2, NLAT, NLON), factor)
```

```python
import functools
import math

import jax
import jax.numpy as jnp
from jax import lax
from jax.experimental import pallas as pl
from jax.experimental.pallas import tpu as pltpu
from jax.sharding import PartitionSpec as P

MESH = pl.DeviceIdType.MESH
LANES = 128
SUBS = 8
BLOCK = 8


def iota(shape, dim):
    return lax.broadcasted_iota(jnp.int32, shape, dim)


def dot(left, right, dims):
    return lax.dot_general(
        left,
        right,
        (dims, ((), ())),
        precision=lax.Precision.HIGHEST,
        preferred_element_type=jnp.float32,
    )


def roll(tile, shift):
    shift = shift % LANES
    return tile if shift == 0 else pltpu.roll(tile, shift, 1)


def spread(tile):
    return jnp.broadcast_to(tile, (SUBS, LANES))


def pack_gram(gram):
    n = gram.shape[0]
    return jnp.concatenate([gram[g * SUBS : (g + 1) * SUBS] for g in range(n // SUBS)], axis=1)


def factorize(packed, n):
    groups = n // SUBS
    lane = iota((SUBS, LANES), 1)
    sub = iota((SUBS, LANES), 0)
    rows = []
    for g in range(groups):
        unit = jnp.where(lane == sub + g * SUBS, 1.0, 0.0)
        rows.append(jnp.where(lane < n, unit, roll(packed, n - g * n)))
    pivots = [None] * groups
    for start in range(0, n, BLOCK):
        r = start // SUBS
        columns = [
            [spread(rows[g][:, n + k : n + k + 1]) if g >= r else None for g in range(groups)]
            for k in range(start, start + BLOCK)
        ]
        for step in range(BLOCK):
            k = start + step
            s = k % SUBS
            pivot = spread(columns[step][r][s : s + 1, :])
            pivots[r] = pivot if s == 0 else jnp.where(sub == s, pivot, pivots[r])
            inverse = 1.0 / pivot
            pivot_row = spread(rows[r][s : s + 1, :]) * inverse
            heads = [
                spread(columns[later][r][s : s + 1, :]) * inverse for later in range(step + 1, BLOCK)
            ]
            for g in range(r, groups):
                factor = columns[step][g]
                if g == r:
                    if s == SUBS - 1:
                        continue
                    factor = jnp.where(sub > s, factor, 0.0)
                rows[g] = rows[g] - factor * pivot_row
                for later in range(step + 1, BLOCK):
                    columns[later][g] = columns[later][g] - factor * heads[later - step - 1]
    out = []
    for g in range(groups):
        scaled = rows[g] * (1.0 / jnp.sqrt(pivots[g]))
        keep = (lane < n) | (lane - n >= sub + g * SUBS)
        out.append(jnp.where(keep, scaled, 0.0))
    return jnp.concatenate(out, axis=0)


def kernel(
    sizes,
    u_ref,
    v_ref,
    modes_ref,
    factor_ref,
    x_ref,
    lat_out,
    lat_in,
    lon_out,
    lon_in,
    first_buf,
    second_buf,
    lat_send,
    lat_recv,
    lon_send,
    lon_recv,
    first_send,
    first_recv,
    second_send,
    second_recv,
):
    lat_size, lon_size, cores = sizes
    snaps, cells, width = u_ref.shape
    depth = lon_size // cores
    members = lat_size * cores
    lat = lax.axis_index("lat")
    lon = lax.axis_index("lon")
    z = lon // cores
    core = lon % cores
    mine = lat * cores + core
    lat_up = (lat + 1) % lat_size
    lat_down = (lat + lat_size - 1) % lat_size
    east = (lon + 1) % lon_size
    west = (lon + lon_size - 1) % lon_size

    def member(d):
        other = (mine + d) % members
        return other, (other // cores, z * cores + other % cores)

    def plane(d):
        other = (z + d) % depth
        return other, (lat, other * cores + core)

    barrier = pltpu.get_barrier_semaphore()
    peers = [member(d)[1] for d in range(1, members)] + [plane(d)[1] for d in range(1, depth)]
    peers += [(lat, east), (lat, west)]
    for peer in peers:
        pl.semaphore_signal(barrier, inc=1, device_id=peer, device_id_type=MESH)

    lane = iota((SUBS, LANES), 1)
    fields = (u_ref, v_ref)
    parts = snaps // SUBS
    winds = [[ref[:, i, :] for i in range(cells)] for ref in fields]
    for f in range(2):
        lat_out[0, f] = winds[f][cells - 1]
        lat_out[1, f] = winds[f][0]
    edge = jnp.zeros((SUBS, LANES), jnp.float32)
    for f in range(2):
        for i in range(cells):
            for t in range(parts):
                q = (f * cells + i) * parts + t
                tile = winds[f][i][t * SUBS : (t + 1) * SUBS]
                edge = jnp.where(lane // 2 == q, roll(tile, 2 * q + 1), edge)
    lon_out[...] = edge

    pl.semaphore_wait(barrier, len(peers))

    copies = []
    for way, target in ((0, lat_up), (1, lat_down)):
        copies.append(
            pltpu.make_async_remote_copy(
                src_ref=lat_out.at[way],
                dst_ref=lat_in.at[way],
                send_sem=lat_send.at[way],
                recv_sem=lat_recv.at[way],
                device_id=(target, lon),
                device_id_type=MESH,
            )
        )
    for way, target in ((0, east), (1, west)):
        copies.append(
            pltpu.make_async_remote_copy(
                src_ref=lon_out,
                dst_ref=lon_in.at[way],
                send_sem=lon_send.at[way],
                recv_sem=lon_recv.at[way],
                device_id=(lat, target),
                device_id_type=MESH,
            )
        )
    for copy in copies:
        copy.start()

    nlat = lat_size * cells
    step = 2.0 * math.pi / (lon_size * width)
    row_index = lat * cells - 1 + iota((2 * SUBS, LANES), 0)
    cosines = jnp.cos((row_index.astype(jnp.float32) + 0.5 - nlat / 2) * step)
    weights = jnp.where((row_index >= 0) & (row_index < nlat), cosines, 0.0)
    scales = 0.5 / jnp.sqrt(cosines)

    def weight(i):
        return weights[i + 1 : i + 2, :]

    def scale(i):
        return scales[i + 1 : i + 2, :]

    wide = iota((snaps, LANES), 1)

    def lon_inner(tile):
        right = jnp.where(wide == LANES - 1, 0.0, pltpu.roll(tile, LANES - 1, 1))
        return right - jnp.where(wide == 0, 0.0, pltpu.roll(tile, 1, 1))

    def lat_inner(f, i):
        high = weight(i + 1) * winds[f][i + 1] if i + 1 < cells else 0.0
        low = weight(i - 1) * winds[f][i - 1] if i > 0 else 0.0
        return high - low

    for i in range(cells):
        x_ref[i] = lon_inner(winds[1][i]) - lat_inner(0, i)
        x_ref[cells + i] = lon_inner(winds[0][i]) + lat_inner(1, i)

    for copy in copies:
        copy.wait_recv()

    ends = jnp.where(lane % 2 == 1, roll(lon_in[0], 1), roll(lon_in[1], LANES - 1))
    sign = jnp.where(lane == LANES - 1, 1.0, jnp.where(lane == 0, -1.0, 0.0))

    def lon_edge(f, i):
        pieces = []
        for t in range(parts):
            q = (f * cells + i) * parts + t
            pieces.append(sign * roll(ends, -(2 * q + 1)))
        return jnp.concatenate(pieces, axis=0)

    def lat_edge(f, i):
        total = 0.0
        if i == cells - 1:
            total = total + weight(cells) * lat_in[1, f]
        if i == 0:
            total = total - weight(-1) * lat_in[0, f]
        return total

    columns = []
    for i in range(cells):
        columns.append((x_ref[i] + lon_edge(1, i) - lat_edge(0, i)) * scale(i))
    for i in range(cells):
        columns.append((x_ref[cells + i] + lon_edge(0, i) + lat_edge(1, i)) * scale(i))
    block = jnp.concatenate(columns, axis=1)

    pending = []

    def exchange(buf, slot, count, peer_of, send, recv, at, value):
        buf[at, slot] = value
        for d in range(1, count):
            other, peer = peer_of(d)
            copy = pltpu.make_async_remote_copy(
                src_ref=buf.at[at, slot],
                dst_ref=buf.at[at, slot],
                send_sem=send.at[at, d - 1],
                recv_sem=recv.at[at, slot],
                device_id=peer,
                device_id_type=MESH,
            )
            copy.start()
            pending.append(copy)
        for d in range(1, count):
            other, peer = peer_of(d)
            pltpu.make_async_remote_copy(
                src_ref=buf.at[at, other],
                dst_ref=buf.at[at, other],
                send_sem=send.at[at, d - 1],
                recv_sem=recv.at[at, other],
                device_id=peer,
                device_id_type=MESH,
            ).wait_recv()
        total = buf[at, 0]
        for index in range(1, count):
            total = total + buf[at, index]
        return total

    def merged(value, at):
        value = exchange(first_buf, mine, members, member, first_send, first_recv, at, value)
        return exchange(second_buf, z, depth, plane, second_send, second_recv, at, value)

    root = math.sqrt(2 * nlat * lon_size * width)
    gram = dot(block, block, ((1,), (1,)))
    first = factorize(merged(pack_gram(gram), 0), snaps)
    solved = dot(first[:, :snaps], block, ((1,), (0,)))
    gram = dot(solved, solved, ((1,), (1,)))
    second = factorize(merged(pack_gram(gram), 1), snaps)
    modes = dot(second[:, :snaps] * root, solved, ((1,), (0,)))
    for f in range(2):
        for i in range(cells):
            at = (f * cells + i) * width
            modes_ref[:, f, i, :] = modes[:, at : at + width]
    upper = [pltpu.roll(m, LANES - snaps, 1)[:, :snaps] for m in (second, first)]
    factor_ref[...] = dot(upper[0], upper[1], ((1,), (0,))) / root

    for copy in copies + pending:
        copy.wait_send()


def shards(sizes, wind_u, wind_v):
    snaps, cells, width = wind_u.shape
    lat_size, lon_size, cores = sizes
    members, depth = lat_size * cores, lon_size // cores
    f32 = jnp.float32
    dma = pltpu.SemaphoreType.DMA
    vmem = pl.BlockSpec(memory_space=pltpu.VMEM)
    return pl.pallas_call(
        functools.partial(kernel, sizes),
        out_shape=(
            jax.ShapeDtypeStruct((snaps, 2, cells, width), f32),
            jax.ShapeDtypeStruct((snaps, snaps), f32),
        ),
        in_specs=[vmem, vmem],
        out_specs=(vmem, vmem),
        scratch_shapes=[
            pltpu.VMEM((2 * cells, snaps, width), f32),
            pltpu.VMEM((2, 2, snaps, width), f32),
            pltpu.VMEM((2, 2, snaps, width), f32),
            pltpu.VMEM((SUBS, LANES), f32),
            pltpu.VMEM((2, SUBS, LANES), f32),
            pltpu.VMEM((2, members, SUBS, LANES), f32),
            pltpu.VMEM((2, depth, SUBS, LANES), f32),
            dma((2,)),
            dma((2,)),
            dma((2,)),
            dma((2,)),
            dma((2, members)),
            dma((2, members)),
            dma((2, depth)),
            dma((2, depth)),
        ],
        compiler_params=pltpu.CompilerParams(collective_id=0, has_side_effects=True),
    )(wind_u, wind_v)


def solution(mesh):
    lat_size, lon_size = mesh.shape["lat"], mesh.shape["lon"]
    sizes = (lat_size, lon_size, 2 if lon_size % 2 == 0 else 1)
    in_specs = (P(None, "lat", "lon"), P(None, "lat", "lon"))
    out_specs = (P(None, None, "lat", "lon"), P())
    return jax.shard_map(
        functools.partial(shards, sizes),
        mesh=mesh,
        in_specs=in_specs,
        out_specs=out_specs,
        check_vma=False,
    )
```

```python
import functools
import math

import jax
import jax.numpy as jnp
from jax import lax
from jax.experimental import pallas as pl
from jax.experimental.pallas import tpu as pltpu
from jax.sharding import PartitionSpec as P

MESH = pl.DeviceIdType.MESH
LANES = 128
SUBS = 8
BLOCK = 8


def iota(shape, dim):
    return lax.broadcasted_iota(jnp.int32, shape, dim)


def dot(left, right, dims):
    return lax.dot_general(
        left,
        right,
        (dims, ((), ())),
        precision=lax.Precision.HIGHEST,
        preferred_element_type=jnp.float32,
    )


def roll(tile, shift):
    shift = shift % LANES
    return tile if shift == 0 else pltpu.roll(tile, shift, 1)


def spread(tile):
    return jnp.broadcast_to(tile, (SUBS, LANES))


def pack_gram(gram):
    n = gram.shape[0]
    return jnp.concatenate([gram[g * SUBS : (g + 1) * SUBS] for g in range(n // SUBS)], axis=1)


def factorize(packed, n):
    groups = n // SUBS
    lane = iota((SUBS, LANES), 1)
    sub = iota((SUBS, LANES), 0)
    rows = []
    for g in range(groups):
        unit = jnp.where(lane == sub + g * SUBS, 1.0, 0.0)
        rows.append(jnp.where(lane < n, unit, roll(packed, n - g * n)))
    pivots = [None] * groups
    for start in range(0, n, BLOCK):
        r = start // SUBS
        columns = [
            [spread(rows[g][:, n + k : n + k + 1]) if g >= r else None for g in range(groups)]
            for k in range(start, start + BLOCK)
        ]
        for step in range(BLOCK):
            k = start + step
            s = k % SUBS
            pivot = spread(columns[step][r][s : s + 1, :])
            pivots[r] = pivot if s == 0 else jnp.where(sub == s, pivot, pivots[r])
            inverse = 1.0 / pivot
            pivot_row = spread(rows[r][s : s + 1, :]) * inverse
            heads = [
                spread(columns[later][r][s : s + 1, :]) * inverse for later in range(step + 1, BLOCK)
            ]
            for g in range(r, groups):
                factor = columns[step][g]
                if g == r:
                    if s == SUBS - 1:
                        continue
                    factor = jnp.where(sub > s, factor, 0.0)
                rows[g] = rows[g] - factor * pivot_row
                for later in range(step + 1, BLOCK):
                    columns[later][g] = columns[later][g] - factor * heads[later - step - 1]
    out = []
    for g in range(groups):
        scaled = rows[g] * (1.0 / jnp.sqrt(pivots[g]))
        keep = (lane < n) | (lane - n >= sub + g * SUBS)
        out.append(jnp.where(keep, scaled, 0.0))
    return jnp.concatenate(out, axis=0)


def kernel(
    sizes,
    u_hbm,
    v_hbm,
    solved_ref,
    first_ref,
    second_ref,
    wind_ref,
    x_ref,
    lat_out,
    lat_in,
    lon_out,
    lon_in,
    pair_buf,
    chip_buf,
    lat_send,
    lat_recv,
    lon_send,
    lon_recv,
    pair_send,
    pair_recv,
    chip_send,
    chip_recv,
    local_sem,
):
    lat_size, lon_size, cores = sizes
    _, snaps, cells, width = wind_ref.shape
    depth = lon_size // cores
    chips = lat_size * depth
    lat = lax.axis_index("lat")
    lon = lax.axis_index("lon")
    z = lon // cores
    core = lon % cores
    mine = lat * depth + z
    lat_up = (lat + 1) % lat_size
    lat_down = (lat + lat_size - 1) % lat_size
    east = (lon + 1) % lon_size
    west = (lon + lon_size - 1) % lon_size

    def twin(d):
        other = (core + d) % cores
        return other, (lat, z * cores + other)

    def chip(d):
        other = (mine + d) % chips
        return other, (other // depth, (other % depth) * cores + core)

    barrier = pltpu.get_barrier_semaphore()
    peers = [chip(d)[1] for d in range(1, chips)] + [twin(d)[1] for d in range(1, cores)]
    peers += [(lat, east), (lat, west)]
    for peer in peers:
        pl.semaphore_signal(barrier, inc=1, device_id=peer, device_id_type=MESH)

    loads = [
        pltpu.make_async_copy(hbm, wind_ref.at[f], local_sem.at[f])
        for f, hbm in enumerate((u_hbm, v_hbm))
    ]
    for load in loads:
        load.start()
    for load in loads:
        load.wait()

    lane = iota((SUBS, LANES), 1)
    parts = snaps // SUBS
    winds = [[wind_ref[f, :, i, :] for i in range(cells)] for f in range(2)]
    for f in range(2):
        lat_out[0, f] = winds[f][cells - 1]
        lat_out[1, f] = winds[f][0]
    edge = jnp.zeros((SUBS, LANES), jnp.float32)
    for f in range(2):
        for i in range(cells):
            for t in range(parts):
                q = (f * cells + i) * parts + t
                tile = winds[f][i][t * SUBS : (t + 1) * SUBS]
                edge = jnp.where(lane // 2 == q, roll(tile, 2 * q + 1), edge)
    lon_out[...] = edge

    pl.semaphore_wait(barrier, len(peers))

    copies = []
    for way, target in ((0, lat_up), (1, lat_down)):
        copies.append(
            pltpu.make_async_remote_copy(
                src_ref=lat_out.at[way],
                dst_ref=lat_in.at[way],
                send_sem=lat_send.at[way],
                recv_sem=lat_recv.at[way],
                device_id=(target, lon),
                device_id_type=MESH,
            )
        )
    for way, target in ((0, east), (1, west)):
        copies.append(
            pltpu.make_async_remote_copy(
                src_ref=lon_out,
                dst_ref=lon_in.at[way],
                send_sem=lon_send.at[way],
                recv_sem=lon_recv.at[way],
                device_id=(lat, target),
                device_id_type=MESH,
            )
        )
    for at, copy in enumerate(copies):
        if at == 0:
            pl.when(lat < lat_size - 1)(copy.start)
        elif at == 1:
            pl.when(lat > 0)(copy.start)
        else:
            copy.start()

    nlat = lat_size * cells
    step = 2.0 * math.pi / (lon_size * width)
    row_index = lat * cells - 1 + iota((2 * SUBS, LANES), 0)
    cosines = jnp.cos((row_index.astype(jnp.float32) + 0.5 - nlat / 2) * step)
    weights = jnp.where((row_index >= 0) & (row_index < nlat), cosines, 0.0)
    scales = 0.5 / jnp.sqrt(cosines)

    def weight(i):
        return weights[i + 1 : i + 2, :]

    def scale(i):
        return scales[i + 1 : i + 2, :]

    wide = iota((snaps, LANES), 1)

    def lon_inner(tile):
        right = jnp.where(wide == LANES - 1, 0.0, pltpu.roll(tile, LANES - 1, 1))
        return right - jnp.where(wide == 0, 0.0, pltpu.roll(tile, 1, 1))

    def lat_inner(f, i):
        high = weight(i + 1) * winds[f][i + 1] if i + 1 < cells else 0.0
        low = weight(i - 1) * winds[f][i - 1] if i > 0 else 0.0
        return high - low

    for i in range(cells):
        x_ref[i] = lon_inner(winds[1][i]) - lat_inner(0, i)
        x_ref[cells + i] = lon_inner(winds[0][i]) + lat_inner(1, i)

    for at, copy in enumerate(copies):
        if at == 0:
            pl.when(lat > 0)(copy.wait_recv)
        elif at == 1:
            pl.when(lat < lat_size - 1)(copy.wait_recv)
        else:
            copy.wait_recv()

    ends = jnp.where(lane % 2 == 1, roll(lon_in[0], 1), roll(lon_in[1], LANES - 1))
    sign = jnp.where(lane == LANES - 1, 1.0, jnp.where(lane == 0, -1.0, 0.0))

    def lon_edge(f, i):
        pieces = []
        for t in range(parts):
            q = (f * cells + i) * parts + t
            pieces.append(sign * roll(ends, -(2 * q + 1)))
        return jnp.concatenate(pieces, axis=0)

    def lat_edge(f, i):
        total = 0.0
        if i == cells - 1:
            total = total + weight(cells) * lat_in[1, f]
        if i == 0:
            total = total - weight(-1) * lat_in[0, f]
        return total

    columns = []
    for i in range(cells):
        columns.append((x_ref[i] + lon_edge(1, i) - lat_edge(0, i)) * scale(i))
    for i in range(cells):
        columns.append((x_ref[cells + i] + lon_edge(0, i) + lat_edge(1, i)) * scale(i))
    block = jnp.concatenate(columns, axis=1)

    pending = []

    def exchange(buf, slot, count, peer_of, send, recv, at, value):
        buf[at, slot] = value
        for d in range(1, count):
            other, peer = peer_of(d)
            copy = pltpu.make_async_remote_copy(
                src_ref=buf.at[at, slot],
                dst_ref=buf.at[at, slot],
                send_sem=send.at[at, d - 1],
                recv_sem=recv.at[at, slot],
                device_id=peer,
                device_id_type=MESH,
            )
            copy.start()
            pending.append(copy)
        for d in range(1, count):
            other, peer = peer_of(d)
            pltpu.make_async_remote_copy(
                src_ref=buf.at[at, other],
                dst_ref=buf.at[at, other],
                send_sem=send.at[at, d - 1],
                recv_sem=recv.at[at, other],
                device_id=peer,
                device_id_type=MESH,
            ).wait_recv()
        total = buf[at, 0]
        for index in range(1, count):
            total = total + buf[at, index]
        return total

    def merged(value, at):
        value = exchange(pair_buf, core, cores, twin, pair_send, pair_recv, at, value)
        return exchange(chip_buf, mine, chips, chip, chip_send, chip_recv, at, value)

    gram = dot(block, block, ((1,), (1,)))
    first = factorize(merged(pack_gram(gram), 0), snaps)
    first_ref[...] = first
    solved = dot(first[:, :snaps], block, ((1,), (0,)))
    solved_ref[...] = solved
    gram = dot(solved, solved, ((1,), (1,)))
    second_ref[...] = factorize(merged(pack_gram(gram), 1), snaps)

    for at, copy in enumerate(copies + pending):
        if at == 0:
            pl.when(lat < lat_size - 1)(copy.wait_send)
        elif at == 1:
            pl.when(lat > 0)(copy.wait_send)
        else:
            copy.wait_send()


def finish(root, solved_ref, first_ref, second_ref, modes_ref, factor_ref):
    snaps, _, cells, width = modes_ref.shape
    first, second = first_ref[...], second_ref[...]
    modes = dot(second[:, :snaps] * root, solved_ref[...], ((1,), (0,)))
    for f in range(2):
        for i in range(cells):
            at = (f * cells + i) * width
            modes_ref[:, f, i, :] = modes[:, at : at + width]
    upper = [pltpu.roll(m, LANES - snaps, 1)[:, :snaps] for m in (second, first)]
    factor_ref[...] = dot(upper[0], upper[1], ((1,), (0,))) / root


def shards(sizes, wind_u, wind_v):
    snaps, cells, width = wind_u.shape
    lat_size, lon_size, cores = sizes
    chips = lat_size * lon_size // cores
    f32 = jnp.float32
    dma = pltpu.SemaphoreType.DMA
    vmem = pl.BlockSpec(memory_space=pltpu.VMEM)
    anywhere = pl.BlockSpec(memory_space=pl.ANY)
    held = pl.pallas_call(
        functools.partial(kernel, sizes),
        out_shape=(
            jax.ShapeDtypeStruct((snaps, 2 * cells * width), f32),
            jax.ShapeDtypeStruct((snaps, LANES), f32),
            jax.ShapeDtypeStruct((snaps, LANES), f32),
        ),
        in_specs=[anywhere, anywhere],
        out_specs=(vmem, vmem, vmem),
        scratch_shapes=[
            pltpu.VMEM((2, snaps, cells, width), f32),
            pltpu.VMEM((2 * cells, snaps, width), f32),
            pltpu.VMEM((2, 2, snaps, width), f32),
            pltpu.VMEM((2, 2, snaps, width), f32),
            pltpu.VMEM((SUBS, LANES), f32),
            pltpu.VMEM((2, SUBS, LANES), f32),
            pltpu.VMEM((2, cores, SUBS, LANES), f32),
            pltpu.VMEM((2, chips, SUBS, LANES), f32),
            dma((2,)),
            dma((2,)),
            dma((2,)),
            dma((2,)),
            dma((2, cores)),
            dma((2, cores)),
            dma((2, chips)),
            dma((2, chips)),
            dma((2,)),
        ],
        compiler_params=pltpu.CompilerParams(collective_id=0, has_side_effects=True),
    )(wind_u, wind_v)
    root = math.sqrt(2 * lat_size * cells * lon_size * width)
    return pl.pallas_call(
        functools.partial(finish, root),
        out_shape=(
            jax.ShapeDtypeStruct((snaps, 2, cells, width), f32),
            jax.ShapeDtypeStruct((snaps, snaps), f32),
        ),
        in_specs=[vmem, vmem, vmem],
        out_specs=(vmem, vmem),
    )(*held)


def solution(mesh):
    lat_size, lon_size = mesh.shape["lat"], mesh.shape["lon"]
    sizes = (lat_size, lon_size, 2 if lon_size % 2 == 0 else 1)
    in_specs = (P(None, "lat", "lon"), P(None, "lat", "lon"))
    out_specs = (P(None, None, "lat", "lon"), P())
    return jax.shard_map(
        functools.partial(shards, sizes),
        mesh=mesh,
        in_specs=in_specs,
        out_specs=out_specs,
        check_vma=False,
    )
```

```python
import functools
import math

import jax
import jax.numpy as jnp
from jax import lax
from jax.experimental import pallas as pl
from jax.experimental.pallas import tpu as pltpu
from jax.sharding import PartitionSpec as P

MESH = pl.DeviceIdType.MESH
LANES = 128
SUBS = 8
BLOCK = 8
VMEM_BYTES = 8 * 1024 * 1024


def iota(shape, dim):
    return lax.broadcasted_iota(jnp.int32, shape, dim)


def dot(left, right, dims):
    return lax.dot_general(
        left,
        right,
        (dims, ((), ())),
        precision=lax.Precision.HIGHEST,
        preferred_element_type=jnp.float32,
    )


def roll(tile, shift):
    shift = shift % LANES
    return tile if shift == 0 else pltpu.roll(tile, shift, 1)


def spread(tile):
    return jnp.broadcast_to(tile, (SUBS, LANES))


def pack_gram(gram):
    n = gram.shape[0]
    return jnp.concatenate([gram[g * SUBS : (g + 1) * SUBS] for g in range(n // SUBS)], axis=1)


def factorize(packed, n):
    groups = n // SUBS
    lane = iota((SUBS, LANES), 1)
    sub = iota((SUBS, LANES), 0)
    rows = []
    for g in range(groups):
        unit = jnp.where(lane == sub + g * SUBS, 1.0, 0.0)
        rows.append(jnp.where(lane < n, unit, roll(packed, n - g * n)))
    pivots = [None] * groups
    for start in range(0, n, BLOCK):
        r = start // SUBS
        columns = [
            [spread(rows[g][:, n + k : n + k + 1]) if g >= r else None for g in range(groups)]
            for k in range(start, start + BLOCK)
        ]
        for step in range(BLOCK):
            k = start + step
            s = k % SUBS
            pivot = spread(columns[step][r][s : s + 1, :])
            pivots[r] = pivot if s == 0 else jnp.where(sub == s, pivot, pivots[r])
            inverse = 1.0 / pivot
            pivot_row = spread(rows[r][s : s + 1, :]) * inverse
            heads = [
                spread(columns[later][r][s : s + 1, :]) * inverse for later in range(step + 1, BLOCK)
            ]
            for g in range(r, groups):
                factor = columns[step][g]
                if g == r:
                    if s == SUBS - 1:
                        continue
                    factor = jnp.where(sub > s, factor, 0.0)
                rows[g] = rows[g] - factor * pivot_row
                for later in range(step + 1, BLOCK):
                    columns[later][g] = columns[later][g] - factor * heads[later - step - 1]
    out = []
    for g in range(groups):
        scaled = rows[g] * (1.0 / jnp.sqrt(pivots[g]))
        keep = (lane < n) | (lane - n >= sub + g * SUBS)
        out.append(jnp.where(keep, scaled, 0.0))
    return jnp.concatenate(out, axis=0)


def kernel(
    sizes,
    u_hbm,
    v_hbm,
    solved_ref,
    first_ref,
    second_ref,
    wind_ref,
    x_ref,
    lat_out,
    lat_in,
    lon_out,
    lon_in,
    pair_buf,
    chip_buf,
    lat_send,
    lat_recv,
    lon_send,
    lon_recv,
    pair_send,
    pair_recv,
    chip_send,
    chip_recv,
    relay_sem,
    local_sem,
):
    lat_size, lon_size, cores = sizes
    _, snaps, cells, width = wind_ref.shape
    depth = lon_size // cores
    chips = lat_size * depth
    lat = lax.axis_index("lat")
    lon = lax.axis_index("lon")
    z = lon // cores
    core = lon % cores
    mine = lat * depth + z
    lat_up = (lat + 1) % lat_size
    lat_down = (lat + lat_size - 1) % lat_size
    east = (lon + 1) % lon_size
    west = (lon + lon_size - 1) % lon_size

    def twin(d):
        other = (core + d) % cores
        return other, (lat, z * cores + other)

    def chip(d):
        other = (mine + d) % chips
        return other, (other // depth, (other % depth) * cores + core)

    barrier = pltpu.get_barrier_semaphore()
    def along(d):
        return [(lat, (z + depth + s) % depth * cores + core) for s in (d, -d)]

    strides = relay_strides(depth)
    peers = [
        ((lat + a) % lat_size, z * cores + (core + b) % cores)
        for a in range(lat_size)
        for b in range(cores)
        if a or b
    ]
    peers += [(lat, east), (lat, west)] + (along(1) if depth > 1 else [])
    for peer in peers:
        pl.semaphore_signal(barrier, inc=1, device_id=peer, device_id_type=MESH)

    loads = [
        pltpu.make_async_copy(hbm, wind_ref.at[f], local_sem.at[f])
        for f, hbm in enumerate((u_hbm, v_hbm))
    ]
    for load in loads:
        load.start()
    for load in loads:
        load.wait()

    lane = iota((SUBS, LANES), 1)
    parts = snaps // SUBS
    winds = [[wind_ref[f, :, i, :] for i in range(cells)] for f in range(2)]
    for f in range(2):
        lat_out[0, f] = winds[f][cells - 1]
        lat_out[1, f] = winds[f][0]
    edge = jnp.zeros((SUBS, LANES), jnp.float32)
    for f in range(2):
        for i in range(cells):
            for t in range(parts):
                q = (f * cells + i) * parts + t
                tile = winds[f][i][t * SUBS : (t + 1) * SUBS]
                edge = jnp.where(lane // 2 == q, roll(tile, 2 * q + 1), edge)
    lon_out[...] = edge

    pl.semaphore_wait(barrier, len(peers))

    copies = []
    for way, target in ((0, lat_up), (1, lat_down)):
        copies.append(
            pltpu.make_async_remote_copy(
                src_ref=lat_out.at[way],
                dst_ref=lat_in.at[way],
                send_sem=lat_send.at[way],
                recv_sem=lat_recv.at[way],
                device_id=(target, lon),
                device_id_type=MESH,
            )
        )
    for way, target in ((0, east), (1, west)):
        copies.append(
            pltpu.make_async_remote_copy(
                src_ref=lon_out,
                dst_ref=lon_in.at[way],
                send_sem=lon_send.at[way],
                recv_sem=lon_recv.at[way],
                device_id=(lat, target),
                device_id_type=MESH,
            )
        )
    for at, copy in enumerate(copies):
        if at == 0:
            pl.when(lat < lat_size - 1)(copy.start)
        elif at == 1:
            pl.when(lat > 0)(copy.start)
        else:
            copy.start()

    def relay(at):
        for peer in along(strides[at]):
            pl.semaphore_signal(relay_sem.at[at], inc=1, device_id=peer, device_id_type=MESH)

    if strides:
        relay(0)

    nlat = lat_size * cells
    step = 2.0 * math.pi / (lon_size * width)
    row_index = lat * cells - 1 + iota((2 * SUBS, LANES), 0)
    cosines = jnp.cos((row_index.astype(jnp.float32) + 0.5 - nlat / 2) * step)
    weights = jnp.where((row_index >= 0) & (row_index < nlat), cosines, 0.0)
    scales = 0.5 / jnp.sqrt(cosines)

    def weight(i):
        return weights[i + 1 : i + 2, :]

    def scale(i):
        return scales[i + 1 : i + 2, :]

    wide = iota((snaps, LANES), 1)

    def lon_inner(tile):
        right = jnp.where(wide == LANES - 1, 0.0, pltpu.roll(tile, LANES - 1, 1))
        return right - jnp.where(wide == 0, 0.0, pltpu.roll(tile, 1, 1))

    def lat_inner(f, i):
        high = weight(i + 1) * winds[f][i + 1] if i + 1 < cells else 0.0
        low = weight(i - 1) * winds[f][i - 1] if i > 0 else 0.0
        return high - low

    for i in range(cells):
        x_ref[i] = lon_inner(winds[1][i]) - lat_inner(0, i)
        x_ref[cells + i] = lon_inner(winds[0][i]) + lat_inner(1, i)

    for at in range(1, len(strides)):
        pl.semaphore_wait(relay_sem.at[at - 1], 2)
        relay(at)

    for at, copy in enumerate(copies):
        if at == 0:
            pl.when(lat > 0)(copy.wait_recv)
        elif at == 1:
            pl.when(lat < lat_size - 1)(copy.wait_recv)
        else:
            copy.wait_recv()

    ends = jnp.where(lane % 2 == 1, roll(lon_in[0], 1), roll(lon_in[1], LANES - 1))
    sign = jnp.where(lane == LANES - 1, 1.0, jnp.where(lane == 0, -1.0, 0.0))

    def lon_edge(f, i):
        pieces = []
        for t in range(parts):
            q = (f * cells + i) * parts + t
            pieces.append(sign * roll(ends, -(2 * q + 1)))
        return jnp.concatenate(pieces, axis=0)

    def lat_edge(f, i):
        total = 0.0
        if i == cells - 1:
            total = total + weight(cells) * lat_in[1, f]
        if i == 0:
            total = total - weight(-1) * lat_in[0, f]
        return total

    columns = []
    for i in range(cells):
        columns.append((x_ref[i] + lon_edge(1, i) - lat_edge(0, i)) * scale(i))
    for i in range(cells):
        columns.append((x_ref[cells + i] + lon_edge(0, i) + lat_edge(1, i)) * scale(i))
    block = jnp.concatenate(columns, axis=1)

    pending = []

    def exchange(buf, slot, count, peer_of, send, recv, at, value):
        buf[at, slot] = value
        for d in range(1, count):
            other, peer = peer_of(d)
            copy = pltpu.make_async_remote_copy(
                src_ref=buf.at[at, slot],
                dst_ref=buf.at[at, slot],
                send_sem=send.at[at, d - 1],
                recv_sem=recv.at[at, slot],
                device_id=peer,
                device_id_type=MESH,
            )
            copy.start()
            pending.append(copy)
        for d in range(1, count):
            other, peer = peer_of(d)
            pltpu.make_async_remote_copy(
                src_ref=buf.at[at, other],
                dst_ref=buf.at[at, other],
                send_sem=send.at[at, d - 1],
                recv_sem=recv.at[at, other],
                device_id=peer,
                device_id_type=MESH,
            ).wait_recv()
        total = buf[at, 0]
        for index in range(1, count):
            total = total + buf[at, index]
        return total

    def merged(value, at):
        value = exchange(pair_buf, core, cores, twin, pair_send, pair_recv, at, value)
        if at == 0 and strides:
            pl.semaphore_wait(relay_sem.at[len(strides) - 1], 2)
        return exchange(chip_buf, mine, chips, chip, chip_send, chip_recv, at, value)

    gram = dot(block, block, ((1,), (1,)))
    first = factorize(merged(pack_gram(gram), 0), snaps)
    solved = dot(first[:, :snaps], block, ((1,), (0,)))
    gram = dot(solved, solved, ((1,), (1,)))
    solved_ref[...] = solved
    first_ref[...] = first
    second_ref[...] = factorize(merged(pack_gram(gram), 1), snaps)

    for at, copy in enumerate(copies + pending):
        if at == 0:
            pl.when(lat < lat_size - 1)(copy.wait_send)
        elif at == 1:
            pl.when(lat > 0)(copy.wait_send)
        else:
            copy.wait_send()


def finish(root, solved_ref, first_ref, second_ref, modes_ref, factor_ref):
    snaps, _, cells, width = modes_ref.shape
    first, second = first_ref[...], second_ref[...]
    modes = dot(second[:, :snaps] * root, solved_ref[...], ((1,), (0,)))
    for f in range(2):
        for i in range(cells):
            at = (f * cells + i) * width
            modes_ref[:, f, i, :] = modes[:, at : at + width]
    upper = [pltpu.roll(m, LANES - snaps, 1)[:, :snaps] for m in (second, first)]
    factor_ref[...] = dot(upper[0], upper[1], ((1,), (0,))) / root


def relay_strides(depth):
    strides, reach = [], 0
    while reach < depth // 2:
        strides.append(max(reach, 1))
        reach += strides[-1]
    return strides


def shards(sizes, wind_u, wind_v):
    snaps, cells, width = wind_u.shape
    lat_size, lon_size, cores = sizes
    chips = lat_size * lon_size // cores
    f32 = jnp.float32
    dma = pltpu.SemaphoreType.DMA
    vmem = pl.BlockSpec(memory_space=pltpu.VMEM)
    hbm = pl.BlockSpec(memory_space=pltpu.HBM)
    held = pl.pallas_call(
        functools.partial(kernel, sizes),
        out_shape=(
            pltpu.VMEM((snaps, 2 * cells * width), f32),
            pltpu.VMEM((snaps, LANES), f32),
            pltpu.VMEM((snaps, LANES), f32),
        ),
        in_specs=[hbm, hbm],
        out_specs=(vmem, vmem, vmem),
        scratch_shapes=[
            pltpu.VMEM((2, snaps, cells, width), f32),
            pltpu.VMEM((2 * cells, snaps, width), f32),
            pltpu.VMEM((2, 2, snaps, width), f32),
            pltpu.VMEM((2, 2, snaps, width), f32),
            pltpu.VMEM((SUBS, LANES), f32),
            pltpu.VMEM((2, SUBS, LANES), f32),
            pltpu.VMEM((2, cores, SUBS, LANES), f32),
            pltpu.VMEM((2, chips, SUBS, LANES), f32),
            dma((2,)),
            dma((2,)),
            dma((2,)),
            dma((2,)),
            dma((2, cores)),
            dma((2, cores)),
            dma((2, chips)),
            dma((2, chips)),
            pltpu.SemaphoreType.REGULAR((max(len(relay_strides(lon_size // cores)), 1),)),
            dma((2,)),
        ],
        compiler_params=pltpu.CompilerParams(
            collective_id=0, has_side_effects=True, vmem_limit_bytes=VMEM_BYTES
        ),
    )(*(pltpu.with_memory_space_constraint(w, pltpu.HBM) for w in (wind_u, wind_v)))
    root = math.sqrt(2 * lat_size * cells * lon_size * width)
    return pl.pallas_call(
        functools.partial(finish, root),
        out_shape=(
            jax.ShapeDtypeStruct((snaps, 2, cells, width), f32),
            jax.ShapeDtypeStruct((snaps, snaps), f32),
        ),
        in_specs=[vmem, vmem, vmem],
        out_specs=(vmem, vmem),
        compiler_params=pltpu.CompilerParams(vmem_limit_bytes=VMEM_BYTES),
    )(*held)


def solution(mesh):
    lat_size, lon_size = mesh.shape["lat"], mesh.shape["lon"]
    sizes = (lat_size, lon_size, 2 if lon_size % 2 == 0 else 1)
    in_specs = (P(None, "lat", "lon"), P(None, "lat", "lon"))
    out_specs = (P(None, None, "lat", "lon"), P())
    return jax.shard_map(
        functools.partial(shards, sizes),
        mesh=mesh,
        in_specs=in_specs,
        out_specs=out_specs,
        check_vma=False,
    )
```

```python
import functools
import math

import jax
import jax.numpy as jnp
from jax import lax
from jax.experimental import pallas as pl
from jax.experimental.pallas import tpu as pltpu
from jax.sharding import PartitionSpec as P

MESH = pl.DeviceIdType.MESH
LANES = 128
SUBS = 8
BLOCK = 8
VMEM_BYTES = 8 * 1024 * 1024


def iota(shape, dim):
    return lax.broadcasted_iota(jnp.int32, shape, dim)


def dot(left, right, dims):
    return lax.dot_general(
        left,
        right,
        (dims, ((), ())),
        precision=lax.Precision.HIGHEST,
        preferred_element_type=jnp.float32,
    )


def two(tile):
    high = tile.astype(jnp.bfloat16)
    return high, (tile - high.astype(jnp.float32)).astype(jnp.bfloat16)


def pair_dot(left, right, dims):
    a, b = two(left)
    x, y = two(right)

    def one(m, n):
        return lax.dot_general(m, n, (dims, ((), ())), preferred_element_type=jnp.float32)

    return one(a, x) + (one(a, y) + one(b, x))


def roll(tile, shift):
    shift = shift % LANES
    return tile if shift == 0 else pltpu.roll(tile, shift, 1)


def spread(tile):
    return jnp.broadcast_to(tile, (SUBS, LANES))


def pack_gram(gram):
    n = gram.shape[0]
    return jnp.concatenate([gram[g * SUBS : (g + 1) * SUBS] for g in range(n // SUBS)], axis=1)


def factorize(packed, n):
    groups = n // SUBS
    lane = iota((SUBS, LANES), 1)
    sub = iota((SUBS, LANES), 0)
    rows = []
    for g in range(groups):
        unit = jnp.where(lane == sub + g * SUBS, 1.0, 0.0)
        rows.append(jnp.where(lane < n, unit, roll(packed, n - g * n)))
    pivots = [None] * groups
    for start in range(0, n, BLOCK):
        r = start // SUBS
        columns = [
            [spread(rows[g][:, n + k : n + k + 1]) if g >= r else None for g in range(groups)]
            for k in range(start, start + BLOCK)
        ]
        for step in range(BLOCK):
            k = start + step
            s = k % SUBS
            pivot = spread(columns[step][r][s : s + 1, :])
            pivots[r] = pivot if s == 0 else jnp.where(sub == s, pivot, pivots[r])
            inverse = 1.0 / pivot
            pivot_row = spread(rows[r][s : s + 1, :]) * inverse
            heads = [
                spread(columns[later][r][s : s + 1, :]) * inverse for later in range(step + 1, BLOCK)
            ]
            for g in range(r, groups):
                factor = columns[step][g]
                if g == r:
                    if s == SUBS - 1:
                        continue
                    factor = jnp.where(sub > s, factor, 0.0)
                rows[g] = rows[g] - factor * pivot_row
                for later in range(step + 1, BLOCK):
                    columns[later][g] = columns[later][g] - factor * heads[later - step - 1]
    out = []
    for g in range(groups):
        scaled = rows[g] * (1.0 / jnp.sqrt(pivots[g]))
        keep = (lane < n) | (lane - n >= sub + g * SUBS)
        out.append(jnp.where(keep, scaled, 0.0))
    return jnp.concatenate(out, axis=0)


def kernel(
    sizes,
    u_hbm,
    v_hbm,
    solved_ref,
    first_ref,
    second_ref,
    wind_ref,
    x_ref,
    lat_out,
    lat_in,
    lon_out,
    lon_in,
    pair_buf,
    chip_buf,
    lat_send,
    lat_recv,
    lon_send,
    lon_recv,
    pair_send,
    pair_recv,
    chip_send,
    chip_recv,
    relay_sem,
    local_sem,
):
    lat_size, lon_size, cores = sizes
    _, snaps, cells, width = wind_ref.shape
    depth = lon_size // cores
    chips = lat_size * depth
    lat = lax.axis_index("lat")
    lon = lax.axis_index("lon")
    z = lon // cores
    core = lon % cores
    mine = lat * depth + z
    lat_up = (lat + 1) % lat_size
    lat_down = (lat + lat_size - 1) % lat_size
    east = (lon + 1) % lon_size
    west = (lon + lon_size - 1) % lon_size

    def twin(d):
        other = (core + d) % cores
        return other, (lat, z * cores + other)

    def chip(d):
        other = (mine + d) % chips
        return other, (other // depth, (other % depth) * cores + core)

    barrier = pltpu.get_barrier_semaphore()
    def along(d):
        return [(lat, (z + depth + s) % depth * cores + core) for s in (d, -d)]

    strides = relay_strides(depth)
    peers = [
        ((lat + a) % lat_size, z * cores + (core + b) % cores)
        for a in range(lat_size)
        for b in range(cores)
        if a or b
    ]
    peers += [(lat, east), (lat, west)] + (along(1) if depth > 1 else [])
    for peer in peers:
        pl.semaphore_signal(barrier, inc=1, device_id=peer, device_id_type=MESH)

    loads = [
        pltpu.make_async_copy(hbm, wind_ref.at[f], local_sem.at[f])
        for f, hbm in enumerate((u_hbm, v_hbm))
    ]
    for load in loads:
        load.start()
    for load in loads:
        load.wait()

    lane = iota((SUBS, LANES), 1)
    parts = snaps // SUBS
    winds = [[wind_ref[f, :, i, :] for i in range(cells)] for f in range(2)]
    for f in range(2):
        lat_out[0, f] = winds[f][cells - 1]
        lat_out[1, f] = winds[f][0]
    edge = jnp.zeros((SUBS, LANES), jnp.float32)
    for f in range(2):
        for i in range(cells):
            for t in range(parts):
                q = (f * cells + i) * parts + t
                tile = winds[f][i][t * SUBS : (t + 1) * SUBS]
                edge = jnp.where(lane // 2 == q, roll(tile, 2 * q + 1), edge)
    lon_out[...] = edge

    pl.semaphore_wait(barrier, len(peers))

    copies = []
    for way, target in ((0, lat_up), (1, lat_down)):
        copies.append(
            pltpu.make_async_remote_copy(
                src_ref=lat_out.at[way],
                dst_ref=lat_in.at[way],
                send_sem=lat_send.at[way],
                recv_sem=lat_recv.at[way],
                device_id=(target, lon),
                device_id_type=MESH,
            )
        )
    for way, target in ((0, east), (1, west)):
        copies.append(
            pltpu.make_async_remote_copy(
                src_ref=lon_out,
                dst_ref=lon_in.at[way],
                send_sem=lon_send.at[way],
                recv_sem=lon_recv.at[way],
                device_id=(lat, target),
                device_id_type=MESH,
            )
        )
    for at, copy in enumerate(copies):
        if at == 0:
            pl.when(lat < lat_size - 1)(copy.start)
        elif at == 1:
            pl.when(lat > 0)(copy.start)
        else:
            copy.start()

    def relay(at):
        for peer in along(strides[at]):
            pl.semaphore_signal(relay_sem.at[at], inc=1, device_id=peer, device_id_type=MESH)

    if strides:
        relay(0)

    nlat = lat_size * cells
    step = 2.0 * math.pi / (lon_size * width)
    row_index = lat * cells - 1 + iota((2 * SUBS, LANES), 0)
    cosines = jnp.cos((row_index.astype(jnp.float32) + 0.5 - nlat / 2) * step)
    weights = jnp.where((row_index >= 0) & (row_index < nlat), cosines, 0.0)
    scales = 0.5 / jnp.sqrt(cosines)

    def weight(i):
        return weights[i + 1 : i + 2, :]

    def scale(i):
        return scales[i + 1 : i + 2, :]

    wide = iota((snaps, LANES), 1)

    def lon_inner(tile):
        right = jnp.where(wide == LANES - 1, 0.0, pltpu.roll(tile, LANES - 1, 1))
        return right - jnp.where(wide == 0, 0.0, pltpu.roll(tile, 1, 1))

    def lat_inner(f, i):
        high = weight(i + 1) * winds[f][i + 1] if i + 1 < cells else 0.0
        low = weight(i - 1) * winds[f][i - 1] if i > 0 else 0.0
        return high - low

    for i in range(cells):
        x_ref[i] = lon_inner(winds[1][i]) - lat_inner(0, i)
        x_ref[cells + i] = lon_inner(winds[0][i]) + lat_inner(1, i)

    for at in range(1, len(strides)):
        pl.semaphore_wait(relay_sem.at[at - 1], 2)
        relay(at)

    for at, copy in enumerate(copies):
        if at == 0:
            pl.when(lat > 0)(copy.wait_recv)
        elif at == 1:
            pl.when(lat < lat_size - 1)(copy.wait_recv)
        else:
            copy.wait_recv()

    ends = jnp.where(lane % 2 == 1, roll(lon_in[0], 1), roll(lon_in[1], LANES - 1))
    sign = jnp.where(lane == LANES - 1, 1.0, jnp.where(lane == 0, -1.0, 0.0))

    def lon_edge(f, i):
        pieces = []
        for t in range(parts):
            q = (f * cells + i) * parts + t
            pieces.append(sign * roll(ends, -(2 * q + 1)))
        return jnp.concatenate(pieces, axis=0)

    def lat_edge(f, i):
        total = 0.0
        if i == cells - 1:
            total = total + weight(cells) * lat_in[1, f]
        if i == 0:
            total = total - weight(-1) * lat_in[0, f]
        return total

    columns = []
    for i in range(cells):
        columns.append((x_ref[i] + lon_edge(1, i) - lat_edge(0, i)) * scale(i))
    for i in range(cells):
        columns.append((x_ref[cells + i] + lon_edge(0, i) + lat_edge(1, i)) * scale(i))
    block = jnp.concatenate(columns, axis=1)

    pending = []

    def exchange(buf, slot, count, peer_of, send, recv, at, value):
        buf[at, slot] = value
        for d in range(1, count):
            other, peer = peer_of(d)
            copy = pltpu.make_async_remote_copy(
                src_ref=buf.at[at, slot],
                dst_ref=buf.at[at, slot],
                send_sem=send.at[at, d - 1],
                recv_sem=recv.at[at, slot],
                device_id=peer,
                device_id_type=MESH,
            )
            copy.start()
            pending.append(copy)
        for d in range(1, count):
            other, peer = peer_of(d)
            pltpu.make_async_remote_copy(
                src_ref=buf.at[at, other],
                dst_ref=buf.at[at, other],
                send_sem=send.at[at, d - 1],
                recv_sem=recv.at[at, other],
                device_id=peer,
                device_id_type=MESH,
            ).wait_recv()
        total = buf[at, 0]
        for index in range(1, count):
            total = total + buf[at, index]
        return total

    def merged(value, at):
        value = exchange(pair_buf, core, cores, twin, pair_send, pair_recv, at, value)
        if at == 0 and strides:
            pl.semaphore_wait(relay_sem.at[len(strides) - 1], 2)
        return exchange(chip_buf, mine, chips, chip, chip_send, chip_recv, at, value)

    gram = dot(block, block, ((1,), (1,)))
    first = factorize(merged(pack_gram(gram), 0), snaps)
    solved = dot(first[:, :snaps], block, ((1,), (0,)))
    gram = pair_dot(solved, solved, ((1,), (1,)))
    solved_ref[...] = solved
    first_ref[...] = first
    second_ref[...] = factorize(merged(pack_gram(gram), 1), snaps)

    for at, copy in enumerate(copies + pending):
        if at == 0:
            pl.when(lat < lat_size - 1)(copy.wait_send)
        elif at == 1:
            pl.when(lat > 0)(copy.wait_send)
        else:
            copy.wait_send()


def finish(root, solved_ref, first_ref, second_ref, modes_ref, factor_ref):
    snaps, _, cells, width = modes_ref.shape
    first, second = first_ref[...], second_ref[...]
    modes = pair_dot(second[:, :snaps] * root, solved_ref[...], ((1,), (0,)))
    for f in range(2):
        for i in range(cells):
            at = (f * cells + i) * width
            modes_ref[:, f, i, :] = modes[:, at : at + width]
    upper = [pltpu.roll(m, LANES - snaps, 1)[:, :snaps] for m in (second, first)]
    factor_ref[...] = dot(upper[0], upper[1], ((1,), (0,))) / root


def relay_strides(depth):
    strides, reach = [], 0
    while reach < depth // 2:
        strides.append(max(reach, 1))
        reach += strides[-1]
    return strides


def shards(sizes, wind_u, wind_v):
    snaps, cells, width = wind_u.shape
    lat_size, lon_size, cores = sizes
    chips = lat_size * lon_size // cores
    f32 = jnp.float32
    dma = pltpu.SemaphoreType.DMA
    vmem = pl.BlockSpec(memory_space=pltpu.VMEM)
    hbm = pl.BlockSpec(memory_space=pltpu.HBM)
    held = pl.pallas_call(
        functools.partial(kernel, sizes),
        out_shape=(
            pltpu.VMEM((snaps, 2 * cells * width), f32),
            pltpu.VMEM((snaps, LANES), f32),
            pltpu.VMEM((snaps, LANES), f32),
        ),
        in_specs=[hbm, hbm],
        out_specs=(vmem, vmem, vmem),
        scratch_shapes=[
            pltpu.VMEM((2, snaps, cells, width), f32),
            pltpu.VMEM((2 * cells, snaps, width), f32),
            pltpu.VMEM((2, 2, snaps, width), f32),
            pltpu.VMEM((2, 2, snaps, width), f32),
            pltpu.VMEM((SUBS, LANES), f32),
            pltpu.VMEM((2, SUBS, LANES), f32),
            pltpu.VMEM((2, cores, SUBS, LANES), f32),
            pltpu.VMEM((2, chips, SUBS, LANES), f32),
            dma((2,)),
            dma((2,)),
            dma((2,)),
            dma((2,)),
            dma((2, cores)),
            dma((2, cores)),
            dma((2, chips)),
            dma((2, chips)),
            pltpu.SemaphoreType.REGULAR((max(len(relay_strides(lon_size // cores)), 1),)),
            dma((2,)),
        ],
        compiler_params=pltpu.CompilerParams(
            collective_id=0, has_side_effects=True, vmem_limit_bytes=VMEM_BYTES
        ),
    )(*(pltpu.with_memory_space_constraint(w, pltpu.HBM) for w in (wind_u, wind_v)))
    root = math.sqrt(2 * lat_size * cells * lon_size * width)
    return pl.pallas_call(
        functools.partial(finish, root),
        out_shape=(
            jax.ShapeDtypeStruct((snaps, 2, cells, width), f32),
            jax.ShapeDtypeStruct((snaps, snaps), f32),
        ),
        in_specs=[vmem, vmem, vmem],
        out_specs=(vmem, vmem),
        compiler_params=pltpu.CompilerParams(vmem_limit_bytes=VMEM_BYTES),
    )(*held)


def solution(mesh):
    lat_size, lon_size = mesh.shape["lat"], mesh.shape["lon"]
    sizes = (lat_size, lon_size, 2 if lon_size % 2 == 0 else 1)
    in_specs = (P(None, "lat", "lon"), P(None, "lat", "lon"))
    out_specs = (P(None, None, "lat", "lon"), P())
    return jax.shard_map(
        functools.partial(shards, sizes),
        mesh=mesh,
        in_specs=in_specs,
        out_specs=out_specs,
        check_vma=False,
    )
```
